32 devices in a mesh: dp: 8 (over y, x, core), ctx: 4 (over z).
Axes of the slice: x: 2, y: 2, z: 4, core: 2. Of those that a mesh axis runs over, the one named last changes fastest.
Arguments:
- query_states: bfloat16 [8, 512, 6144], P('dp', 'ctx'), may hold values from -5 to 5
- key_states: bfloat16 [8, 512, 384], P('dp', 'ctx'), may hold values from -5 to 5
- value_states: bfloat16 [8, 512, 256], P('dp', 'ctx'), may hold values from -6 to 6
- output_grads: bfloat16 [8, 512, 4096], P('dp', 'ctx'), may hold values from -6 to 6
- selection: int32 [8, 8, 2, 8], P('dp', 'ctx'), may hold values from 0 to 7, as said below
- sink_logit: float32 [32], replicated, may hold values from 3 to 7
Outputs:
- query_grad: bfloat16 [8, 512, 6144], P('dp', 'ctx')
- key_grad: bfloat16 [8, 512, 384], P('dp', 'ctx')
- value_grad: bfloat16 [8, 512, 256], P('dp', 'ctx')
- sink_grad: float32 [32], replicated
The draws below stay inside these ranges and needn't reach their ends.
Inputs may be any that keep to these rules, and one draw needn't show every extreme that they name: `selection`: for query block b and group g: slot 0 holds b; the first min(8, b + 1) slots hold distinct blocks not after b; every later slot repeats slot 0.
All inputs are finite; a program needn't handle non-finite values.
Results may differ from the reference program's by a relative error of at most 0.0075.
Values may be sent and summed in bfloat16 or wider, within the bound.
No kernel may reach another device: no remote copies, remote signals or barrier semaphores. Data moves between devices by JAX's collectives and lax.ppermute only.
A program may use at most 128 MiB of HBM per device.

```python
import jax
import jax.numpy as jnp
from jax import lax

G = 2
DK = 192
DV = 128
BLK = 64
TOPN = 8
TOK_DEV = 128
H = 32
SEQS = 8
LEN = 512
NBLK = 8
N_CTX = 4


def drawn_pair(key):
    base = jax.random.fold_in(key, 7)
    query_key, key_key = jax.random.split(base, 2)
    query_f = jax.random.normal(query_key, (SEQS, LEN, H * DK), jnp.float32)
    key_f = jax.random.normal(key_key, (SEQS, LEN, G * DK), jnp.float32)
    return (jnp.clip(query_f, -5.0, 5.0), jnp.clip(key_f, -5.0, 5.0))


def draw_query_states(key, part):
    return drawn_pair(key)[0].astype(jnp.bfloat16)


def draw_key_states(key, part):
    return drawn_pair(key)[1].astype(jnp.bfloat16)


def one_order(item_key):
    return jax.random.permutation(item_key, NBLK).astype(jnp.int32)


def draw_selection(key, part):
    base = jax.random.fold_in(key, 13)
    orders = jax.vmap(one_order)(jax.random.split(base, SEQS * NBLK * G)).reshape(SEQS, NBLK, G, NBLK)
    query_block = jnp.arange(NBLK, dtype=jnp.int32).reshape(1, NBLK, 1, 1)
    candidate = jnp.arange(NBLK, dtype=jnp.int32).reshape(1, 1, 1, NBLK)
    ranking = orders + NBLK * (candidate <= query_block).astype(jnp.int32) + 2 * NBLK * (candidate == query_block).astype(jnp.int32)
    taken = min(TOPN, NBLK)
    best = lax.top_k(ranking, taken)[1].astype(jnp.int32)
    filler = jnp.broadcast_to(best[..., :1], (SEQS, NBLK, G, TOPN - taken))
    padded = jnp.concatenate([best, filler], axis=-1)
    slot = jnp.arange(TOPN, dtype=jnp.int32).reshape(1, 1, 1, TOPN)
    keep = slot < jnp.minimum(TOPN, query_block + 1)
    return jnp.where(keep, padded, padded[..., :1]).astype(jnp.int32)


def shard_levels(key, shape, pieces, least, high):
    loudness, own = 1.0, jax.random.fold_in(key, 6)
    for axis_at, blocks in pieces:
        draws = jnp.exp(jax.random.uniform(jax.random.fold_in(own, axis_at), (blocks,), jnp.float32, least / len(pieces), high / len(pieces)))
        loudness = loudness * jnp.repeat(draws, shape[axis_at] // blocks).reshape([-1 if axis == axis_at else 1 for axis in range(len(shape))])
    return loudness


def normal_values(rng, shape, width, bound, cuts=(), kind=jnp.bfloat16):
    values = width * jax.random.normal(rng, shape, jnp.float32)
    if cuts:
        values = values * shard_levels(rng, shape, cuts, -0.22, 0.18)
    return jnp.clip(values, -bound, bound).astype(kind)


def setup_inputs(seed: int = 0) -> dict:
    arg_keys = jax.random.split(jax.random.key(seed), 7)
    return {
        "query_states": draw_query_states(jax.random.fold_in(arg_keys[6], 71), 0),
        "key_states": draw_key_states(jax.random.fold_in(arg_keys[6], 71), 0),
        "value_states": normal_values(arg_keys[2], (SEQS, LEN, G * DV), 1.0, 6.0, ((0, 8), (1, 4))),
        "output_grads": normal_values(arg_keys[3], (SEQS, LEN, H * DV), 1.0, 6.0, ((0, 8), (1, 4))),
        "selection": draw_selection(jax.random.fold_in(arg_keys[6], 71), 0),
        "sink_logit": jnp.clip(jax.random.uniform(arg_keys[5], (H,), jnp.float32, 3.0, 7.0), 3.0, 7.0),
    }


def block_terms(query_rows, grad_rows, key_whole, value_whole, chosen, block_num, sink_part):
    block_len = query_rows.shape[0]
    head_count = sink_part.shape[0]
    key_width = key_whole.shape[-1]
    value_width = value_whole.shape[-1]
    slot_count = chosen.shape[0]
    score_scale = key_width ** -0.5
    inner_dims = (((1,), (1,)), ((), ()))
    outer_dims = (((0,), (0,)), ((), ()))
    key_sel = jnp.take(key_whole, chosen, axis=0).reshape(slot_count * block_len, key_width)
    value_sel = jnp.take(value_whole, chosen, axis=0).reshape(slot_count * block_len, value_width)
    queries = query_rows.reshape(block_len * head_count, key_width)
    grads = grad_rows.reshape(block_len * head_count, value_width)
    scores = lax.dot_general(queries, key_sel, inner_dims, preferred_element_type=jnp.float32) * score_scale
    scores = scores.reshape(block_len, head_count, slot_count * block_len)
    valid_count = jnp.minimum(slot_count, block_num + 1)
    query_pos = block_num * block_len + jnp.arange(block_len, dtype=jnp.int32)
    key_pos = (chosen[:, None] * block_len + jnp.arange(block_len, dtype=jnp.int32)[None, :]).reshape(-1)
    slot_valid = jnp.repeat(jnp.arange(slot_count, dtype=jnp.int32) < valid_count, block_len)
    allowed = slot_valid[None, :] & (key_pos[None, :] <= query_pos[:, None])
    scores = jnp.where(allowed[:, None, :], scores, -jnp.inf)
    row_max = jnp.maximum(jnp.max(scores, axis=-1), sink_part[None, :])
    exponent = jnp.exp(scores - row_max[..., None])
    sink_term = jnp.exp(sink_part[None, :] - row_max)
    normalizer = sink_term + jnp.sum(exponent, axis=-1)
    probabilities = exponent / normalizer[..., None]
    sink_prob = sink_term / normalizer
    prob_grad = lax.dot_general(grads, value_sel, inner_dims, preferred_element_type=jnp.float32)
    prob_grad = prob_grad.reshape(block_len, head_count, slot_count * block_len)
    row_dot = jnp.sum(probabilities * prob_grad, axis=-1)
    score_grad = (probabilities * (prob_grad - row_dot[..., None])).astype(jnp.bfloat16)
    score_grad = score_grad.reshape(block_len * head_count, slot_count * block_len)
    prob_bf = probabilities.astype(jnp.bfloat16).reshape(block_len * head_count, slot_count * block_len)
    query_grad = jnp.dot(score_grad, key_sel, preferred_element_type=jnp.float32) * score_scale
    query_grad = query_grad.astype(jnp.bfloat16).reshape(block_len, head_count * key_width)
    key_slots = lax.dot_general(score_grad, queries, outer_dims, preferred_element_type=jnp.float32) * score_scale
    value_slots = lax.dot_general(prob_bf, grads, outer_dims, preferred_element_type=jnp.float32)
    sink_grad = -jnp.sum(sink_prob * row_dot, axis=0)
    return (query_grad, key_slots.reshape(slot_count, block_len, key_width),
            value_slots.reshape(slot_count, block_len, value_width), sink_grad)


def device_terms(query_dev, grad_dev, key_whole, value_whole, select_dev, first_block, sink_logit):
    block_total, block_len, group_count, key_width = key_whole.shape
    value_width = value_whole.shape[3]
    head_count = sink_logit.shape[0] // group_count
    block_count = select_dev.shape[0]
    query_blocks = query_dev.reshape(block_count, block_len, group_count, head_count * key_width)
    grad_blocks = grad_dev.reshape(block_count, block_len, group_count, head_count * value_width)

    def per_block(running, inputs):
        key_acc, value_acc, sink_acc = running
        query_blk, grad_blk, chosen_all, block_num = inputs
        grad_parts = []
        sink_parts = []
        for group_id in range(group_count):
            chosen = chosen_all[group_id]
            query_grad, key_slots, value_slots, sink_grad = block_terms(
                query_blk[:, group_id], grad_blk[:, group_id], key_whole[:, :, group_id],
                value_whole[:, :, group_id], chosen, first_block + block_num,
                sink_logit[group_id * head_count:(group_id + 1) * head_count])
            key_acc = key_acc.at[chosen, :, group_id].add(key_slots)
            value_acc = value_acc.at[chosen, :, group_id].add(value_slots)
            grad_parts.append(query_grad)
            sink_parts.append(sink_grad)
        return (key_acc, value_acc, sink_acc + jnp.concatenate(sink_parts)), jnp.stack(grad_parts, axis=1)

    starting = (jnp.zeros((block_total, block_len, group_count, key_width), jnp.float32),
                jnp.zeros((block_total, block_len, group_count, value_width), jnp.float32),
                jnp.zeros((group_count * head_count,), jnp.float32))
    inputs = (query_blocks, grad_blocks, select_dev, jnp.arange(block_count, dtype=jnp.int32))
    (key_acc, value_acc, sink_acc), query_out = lax.scan(per_block, starting, inputs)
    return query_out.reshape(block_count * block_len, -1), key_acc, value_acc, sink_acc


def reference(query_states, key_states, value_states, output_grads, selection, sink_logit):
    block_count = TOK_DEV // BLK

    def per_sequence(items):
        query_seq, key_seq, value_seq, grad_seq, select_seq = items
        key_whole = key_seq.reshape(NBLK, BLK, G, DK)
        value_whole = value_seq.reshape(NBLK, BLK, G, DV)

        def per_device(running, inputs):
            key_total, value_total, sink_total = running
            query_dev, grad_dev, select_dev, device_num = inputs
            query_out, key_acc, value_acc, sink_acc = device_terms(
                query_dev, grad_dev, key_whole, value_whole, select_dev, device_num * block_count, sink_logit)
            key_round = lax.optimization_barrier(key_acc.astype(jnp.bfloat16)).astype(jnp.float32)
            value_round = lax.optimization_barrier(value_acc.astype(jnp.bfloat16)).astype(jnp.float32)
            return (key_total + key_round, value_total + value_round, sink_total + sink_acc), query_out

        starting = (jnp.zeros((NBLK, BLK, G, DK), jnp.float32),
                    jnp.zeros((NBLK, BLK, G, DV), jnp.float32),
                    jnp.zeros((H,), jnp.float32))
        inputs = (query_seq.reshape(N_CTX, TOK_DEV, H * DK), grad_seq.reshape(N_CTX, TOK_DEV, H * DV),
                  select_seq.reshape(N_CTX, block_count, G, TOPN), jnp.arange(N_CTX, dtype=jnp.int32))
        (key_total, value_total, sink_total), query_out = lax.scan(per_device, starting, inputs)
        return (query_out.reshape(LEN, H * DK), key_total.astype(jnp.bfloat16).reshape(LEN, G * DK),
                value_total.astype(jnp.bfloat16).reshape(LEN, G * DV), sink_total)

    query_grad, key_grad, value_grad, sink_parts = lax.map(
        per_sequence, (query_states, key_states, value_states, output_grads, selection))
    return query_grad, key_grad, value_grad, jnp.sum(sink_parts, axis=0)
```

```python
import functools
import math

import jax
import jax.numpy as jnp
from jax import lax
from jax.experimental import pallas as pl
from jax.experimental.pallas import tpu as pltpu
from jax.sharding import PartitionSpec as P

G = 2
DK = 192
DV = 128
BLK = 64
WIDE = 256
SHIFT = WIDE - DK
HEADS_STEP = 4
LOG2E = math.log2(math.e)
OFF = -1e30


LAST = (((1,), (1,)), ((), ()))
FIRST = (((0,), (0,)), ((), ()))


def group_kernel(group, n_chunk, first_head, has_prev, *refs):
    sink_ref, q_ref, do_ref, bias_ref = refs[:4]
    kv_refs = refs[4 : 4 + n_chunk]
    at = 4 + n_chunk + (1 if has_prev else 0)
    dq_ref = refs[at]
    dkv_refs = refs[at + 1 : at + 1 + n_chunk]
    sink_out = refs[at + 1 + n_chunk]
    k_even, k_odd, v_all, dk_even, dk_odd, dv_acc = refs[at + 2 + n_chunk :]
    step = pl.program_id(0)
    tok = q_ref.shape[0]
    score_scale = DK**-0.5

    @pl.when(step == 0)
    def _():
        for d in range(n_chunk):
            rows = slice(d * tok, (d + 1) * tok)
            keys = kv_refs[d][:, DV:]
            pad = jnp.zeros((tok, SHIFT), keys.dtype)
            v_all[rows, :] = kv_refs[d][:, :DV]
            k_even[rows, :] = jnp.concatenate([keys, pad], axis=1)
            k_odd[rows, :] = jnp.concatenate([pad, keys], axis=1)
        dk_even[...] = jnp.zeros_like(dk_even)
        dk_odd[...] = jnp.zeros_like(dk_odd)
        dv_acc[...] = jnp.zeros_like(dv_acc)

    bias = bias_ref[...]
    bias2 = jnp.concatenate([bias, bias], axis=1)
    lane = lax.broadcasted_iota(jnp.int32, (1, 2 * tok), 1)
    dq_parts = []
    dv_sum = None
    for odd in range(2):
        k_all = k_odd if odd else k_even
        dk_acc = dk_odd if odd else dk_even
        c0 = odd * (DK - SHIFT)
        q_rows = jnp.concatenate(
            [q_ref[:, c0 : c0 + WIDE], q_ref[:, 2 * DK + c0 : 2 * DK + c0 + WIDE]], axis=0
        )
        do_rows = jnp.concatenate(
            [
                do_ref[:, odd * DV : (odd + 1) * DV],
                do_ref[:, (2 + odd) * DV : (3 + odd) * DV],
            ],
            axis=0,
        )
        head = first_head + step * HEADS_STEP + odd
        sink = jnp.where(lane < tok, sink_ref[head], sink_ref[head + 2]) * LOG2E
        s = lax.dot_general(k_all[...], q_rows, LAST, preferred_element_type=jnp.float32)
        dp = lax.dot_general(v_all[...], do_rows, LAST, preferred_element_type=jnp.float32)
        s = s * (score_scale * LOG2E) + bias2
        top = jnp.maximum(jnp.max(s, axis=0, keepdims=True), sink)
        e = jnp.exp2(s - top)
        sink_e = jnp.exp2(sink - top)
        total = sink_e + jnp.sum(e, axis=0, keepdims=True)
        inv = 1.0 / total
        dot = jnp.sum(e * dp, axis=0, keepdims=True) * inv
        p = e * inv
        ds = (p * (dp - dot)).astype(jnp.bfloat16)
        p_bf = p.astype(jnp.bfloat16)
        sink_g = -(sink_e * inv) * dot
        sink_out[0, pl.ds(step * HEADS_STEP + odd, 1), :] = sink_g[:, :tok]
        sink_out[0, pl.ds(step * HEADS_STEP + odd + 2, 1), :] = sink_g[:, tok:]
        dv = jnp.dot(p_bf, do_rows, preferred_element_type=jnp.float32)
        dv_sum = dv if dv_sum is None else dv_sum + dv
        dk_acc[...] += jnp.dot(ds, q_rows, preferred_element_type=jnp.float32)
        dq_parts.append(
            lax.dot_general(ds, k_all[...], FIRST, preferred_element_type=jnp.float32)
        )
    dv_acc[...] += dv_sum
    even, odd = dq_parts
    half = WIDE // 2
    for pair in range(2):
        a = even[pair * tok : (pair + 1) * tok]
        b = odd[pair * tok : (pair + 1) * tok]
        base = pair * 2 * DK
        for col, part in ((0, a[:, :half]), (half, a[:, half:] + b[:, :half]), (2 * half, b[:, half:])):
            dq_ref[:, base + col : base + col + half] = (part * score_scale).astype(dq_ref.dtype)

    @pl.when(step == pl.num_programs(0) - 1)
    def _():
        for d in range(n_chunk):
            rows = slice(d * tok, (d + 1) * tok)
            dk = dk_even[rows, :DK] + dk_odd[rows, SHIFT:]
            dkv_refs[d][:, :DV] = dv_acc[rows, :].astype(jnp.bfloat16)
            dkv_refs[d][:, DV:] = (dk * score_scale).astype(jnp.bfloat16)


def run_group(group, sink, q, do, bias, chunks, dq_prev):
    n_chunk = len(chunks)
    tok = q.shape[0]
    heads = sink.shape[0] // G
    steps = heads // HEADS_STEP
    keys = n_chunk * tok
    q_cols, do_cols = HEADS_STEP * DK, HEADS_STEP * DV
    whole = lambda shape: pl.BlockSpec(shape, lambda s: (0,) * len(shape))
    at_group = lambda s: (0, group * steps + s)
    has_prev = dq_prev is not None
    in_specs = [
        pl.BlockSpec(memory_space=pltpu.SMEM),
        pl.BlockSpec((tok, q_cols), at_group),
        pl.BlockSpec((tok, do_cols), at_group),
        pl.BlockSpec((None, keys, tok), lambda s: (group, 0, 0)),
    ] + [whole((tok, DV + DK))] * n_chunk
    args = [sink, q, do, bias] + list(chunks)
    aliases = {}
    if has_prev:
        in_specs.append(pl.BlockSpec(memory_space=pl.ANY))
        args.append(dq_prev)
        aliases = {len(args) - 1: 0}
    out = pl.pallas_call(
        functools.partial(group_kernel, group, n_chunk, group * heads, has_prev),
        grid=(steps,),
        in_specs=in_specs,
        out_specs=[pl.BlockSpec((tok, q_cols), at_group)]
        + [whole((tok, DV + DK))] * n_chunk
        + [whole((1, heads, tok))],
        out_shape=[jax.ShapeDtypeStruct(q.shape, jnp.bfloat16)]
        + [jax.ShapeDtypeStruct((tok, DV + DK), jnp.bfloat16)] * n_chunk
        + [jax.ShapeDtypeStruct((1, heads, tok), jnp.float32)],
        scratch_shapes=[
            pltpu.VMEM((keys, WIDE), jnp.bfloat16),
            pltpu.VMEM((keys, WIDE), jnp.bfloat16),
            pltpu.VMEM((keys, DV), jnp.bfloat16),
            pltpu.VMEM((keys, WIDE), jnp.float32),
            pltpu.VMEM((keys, WIDE), jnp.float32),
            pltpu.VMEM((keys, DV), jnp.float32),
        ],
        input_output_aliases=aliases,
        cost_estimate=pl.CostEstimate(
            flops=2 * keys * tok * heads * (3 * DK + 2 * DV),
            transcendentals=keys * tok * heads,
            bytes_accessed=tok * heads * (4 * DK + 2 * DV) + keys * tok * 4,
        ),
        name=f"group_{group}",
    )(*args)
    return out[0], out[1 : 1 + n_chunk], out[1 + n_chunk]


def make_bias(selection, here, n_ctx, tok):
    blocks, groups, slots = selection.shape
    per = tok // BLK
    dist = jnp.arange(n_ctx, dtype=jnp.int32)
    key_block = (here - dist)[:, None] * per + jnp.arange(per, dtype=jnp.int32)[None, :]
    query_block = here * per + jnp.arange(blocks, dtype=jnp.int32)
    slot_ok = jnp.arange(slots, dtype=jnp.int32)[None, :] < jnp.minimum(slots, query_block + 1)[:, None]
    hit = selection[None, None] == key_block[:, :, None, None, None]
    chosen = jnp.any(hit & slot_ok[None, None, :, None, :], axis=-1)
    chosen = jnp.transpose(chosen, (3, 0, 1, 2))
    chosen = jnp.broadcast_to(
        chosen[:, :, :, None, :, None], (groups, n_ctx, per, BLK, blocks, BLK)
    ).reshape(groups, n_ctx * tok, blocks * BLK)
    key_pos = ((here - dist)[:, None] * tok + jnp.arange(tok, dtype=jnp.int32)[None, :]).reshape(-1)
    query_pos = here * tok + jnp.arange(tok, dtype=jnp.int32)
    causal = key_pos[:, None] <= query_pos[None, :]
    return jnp.where(chosen & causal[None], 0.0, OFF).astype(jnp.float32)


def all_sum(x, sizes):
    for axis, size in sizes:
        if size & (size - 1):
            x = lax.psum(x, axis)
            continue
        hop = 1
        while hop < size:
            x = x + lax.ppermute(x, axis, [(i, i ^ hop) for i in range(size)])
            hop *= 2
    return x


def local(n_dp, n_ctx, query_states, key_states, value_states, output_grads, selection, sink_logit):
    tok = query_states.shape[1]
    here = lax.axis_index("ctx")
    q, k, v, do = query_states[0], key_states[0], value_states[0], output_grads[0]
    gathered = []
    for g in range(G):
        own = jnp.concatenate([v[:, g * DV : (g + 1) * DV], k[:, g * DK : (g + 1) * DK]], axis=1)
        gathered.append(
            [own]
            + [
                lax.ppermute(own, "ctx", [(i, i + d) for i in range(n_ctx - d)])
                for d in range(1, n_ctx)
            ]
        )
    bias = make_bias(selection[0], here, n_ctx, tok)
    dq = None
    sums, sinks = [], []
    for g in range(G):
        dq, parts, sink = run_group(g, sink_logit, q, do, bias, gathered[g], dq)
        total = parts[0].astype(jnp.float32)
        for d in range(1, n_ctx):
            back = lax.ppermute(parts[d], "ctx", [(i, i - d) for i in range(d, n_ctx)])
            total = total + back.astype(jnp.float32)
        sums.append(total.astype(jnp.bfloat16))
        sinks.append(sink)
    key_grad = jnp.concatenate([s[:, DV:] for s in sums], axis=1)
    value_grad = jnp.concatenate([s[:, :DV] for s in sums], axis=1)
    sink = jnp.sum(jnp.concatenate(sinks, axis=1), axis=(0, 2))
    sink = all_sum(sink, (("dp", n_dp), ("ctx", n_ctx)))
    return dq[None], key_grad[None], value_grad[None], sink


def solution(mesh):
    placed = (
        P("dp", "ctx", None),
        P("dp", "ctx", None),
        P("dp", "ctx", None),
        P("dp", "ctx", None),
        P("dp", "ctx", None, None),
        P(),
    )
    return jax.shard_map(
        functools.partial(local, mesh.shape["dp"], mesh.shape["ctx"]),
        mesh=mesh,
        in_specs=placed,
        out_specs=(P("dp", "ctx", None), P("dp", "ctx", None), P("dp", "ctx", None), P()),
        check_vma=False,
    )
```

```python
import functools
import math

import jax
import jax.numpy as jnp
from jax import lax
from jax.experimental import pallas as pl
from jax.experimental.pallas import tpu as pltpu
from jax.sharding import PartitionSpec as P


G = 2
DK = 192
DV = 128
BLK = 64
WIDE = 256
SHIFT = WIDE - DK
HEADS_STEP = 16
CUTS = 4
MCUTS = 1
VMEM_SMALL = 8 * 2**20
VMEM_GROUP = 40 * 2**20
LOG2E = math.log2(math.e)
OFF = -1e30


LAST = (((1,), (1,)), ((), ()))
FIRST = (((0,), (0,)), ((), ()))


def group_kernel(n_chunk, first_head, has_prev, *refs):
    sink_ref, q_ref, do_ref, bias_ref = refs[:4]
    kv_refs = refs[4 : 4 + n_chunk]
    at = 4 + n_chunk + (1 if has_prev else 0)
    dq_ref = refs[at]
    dkv_refs = refs[at + 1 : at + 1 + n_chunk]
    sink_out = refs[at + 1 + n_chunk]
    k_even, k_odd, v_all, dk_even, dk_odd, dv_acc = refs[at + 2 + n_chunk :]
    step = pl.program_id(0)
    tok = q_ref.shape[0]
    score_scale = DK**-0.5

    @pl.when(step == 0)
    def _():
        for d in range(n_chunk):
            rows = slice(d * tok, (d + 1) * tok)
            keys = kv_refs[d][:, DV:]
            pad = jnp.zeros((tok, SHIFT), keys.dtype)
            v_all[rows, :] = kv_refs[d][:, :DV]
            k_even[rows, :] = jnp.concatenate([keys, pad], axis=1)
            k_odd[rows, :] = jnp.concatenate([pad, keys], axis=1)
        dk_even[...] = jnp.zeros_like(dk_even)
        dk_odd[...] = jnp.zeros_like(dk_odd)
        dv_acc[...] = jnp.zeros_like(dv_acc)

    bias = bias_ref[...]
    bias2 = jnp.concatenate([bias, bias], axis=1)
    lane = lax.broadcasted_iota(jnp.int32, (1, 2 * tok), 1)
    half = WIDE // 2
    n_keys = k_even.shape[0]
    span = n_keys // CUTS
    mspan = n_keys // MCUTS
    cuts = [slice(i * span, (i + 1) * span) for i in range(CUTS)]
    mcuts = [slice(i * mspan, (i + 1) * mspan) for i in range(MCUTS)]
    fold = CUTS // MCUTS
    f32 = jnp.float32
    dq_made = {}

    def tile(index):
        quad, odd = divmod(index, 2)
        k_all = k_odd if odd else k_even
        dk_acc = dk_odd if odd else dk_even
        q0 = quad * 4 * DK
        c0 = q0 + odd * (DK - SHIFT)
        o0 = quad * 4 * DV + odd * DV
        row = step * HEADS_STEP + quad * 4 + odd
        head = first_head + row
        t = {"s": [None] * CUTS, "dp": [None] * CUTS, "e": [None] * CUTS,
             "ds": [None] * CUTS, "p": [None] * CUTS}

        def load():
            t["q"] = jnp.concatenate(
                [q_ref[:, c0 : c0 + WIDE], q_ref[:, 2 * DK + c0 : 2 * DK + c0 + WIDE]], axis=0
            )
            t["do"] = jnp.concatenate(
                [do_ref[:, o0 : o0 + DV], do_ref[:, o0 + 2 * DV : o0 + 3 * DV]], axis=0
            )

        def score(i):
            if i == 0:
                load()
            made = lax.dot_general(k_all[mcuts[i], :], t["q"], LAST, preferred_element_type=f32)
            for j in range(fold):
                t["s"][i * fold + j] = made[j * span : (j + 1) * span]

        def grad(i):
            made = lax.dot_general(v_all[mcuts[i], :], t["do"], LAST, preferred_element_type=f32)
            for j in range(fold):
                t["dp"][i * fold + j] = made[j * span : (j + 1) * span]

        def shift(i):
            t["s"][i] = t["s"][i] * (score_scale * LOG2E) + bias2[cuts[i], :]
            top = jnp.max(t["s"][i], axis=0, keepdims=True)
            t["top"] = top if i == 0 else jnp.maximum(t["top"], top)

        def expo(i):
            if i == 0:
                sink = jnp.where(lane < tok, sink_ref[head], sink_ref[head + 2]) * LOG2E
                t["top"] = jnp.maximum(t["top"], sink)
                t["sink_e"] = jnp.exp2(sink - t["top"])
                t["total"] = t["sink_e"]
                t["dot"] = jnp.zeros_like(sink)
            e = jnp.exp2(t["s"][i] - t["top"])
            t["e"][i] = e
            t["total"] += jnp.sum(e, axis=0, keepdims=True)
            t["dot"] += jnp.sum(e * t["dp"][i], axis=0, keepdims=True)

        def finish(i):
            if i == 0:
                t["inv"] = 1.0 / t["total"]
                t["dot"] = t["dot"] * t["inv"]
                sink_g = -(t["sink_e"] * t["inv"]) * t["dot"]
                sink_out[0, pl.ds(row, 1), :] = sink_g[:, :tok]
                sink_out[0, pl.ds(row + 2, 1), :] = sink_g[:, tok:]
            p = t["e"][i] * t["inv"]
            t["p"][i] = p.astype(jnp.bfloat16)
            t["ds"][i] = (p * (t["dp"][i] - t["dot"])).astype(jnp.bfloat16)

        def value(i):
            p = jnp.concatenate(t["p"][i * fold : (i + 1) * fold], axis=0)
            dv_acc[mcuts[i], :] += jnp.dot(p, t["do"], preferred_element_type=f32)

        def key(i):
            ds = jnp.concatenate(t["ds"][i * fold : (i + 1) * fold], axis=0)
            dk_acc[mcuts[i], :] += jnp.dot(ds, t["q"], preferred_element_type=f32)

        def query(pair):
            ds = jnp.concatenate([d[:, pair * tok : (pair + 1) * tok] for d in t["ds"]], axis=0)
            made = lax.dot_general(ds, k_all[...], FIRST, preferred_element_type=f32)
            dq_made[quad, odd, pair] = made
            if not odd:
                return
            a = dq_made.pop((quad, 0, pair))
            b = dq_made.pop((quad, 1, pair))
            base = q0 + pair * 2 * DK
            for col, part in (
                (0, a[:, :half]),
                (half, a[:, half:] + b[:, :half]),
                (2 * half, b[:, half:]),
            ):
                dq_ref[:, base + col : base + col + half] = (part * score_scale).astype(dq_ref.dtype)

        each = range(CUTS)
        wide = range(MCUTS)
        before = [functools.partial(f, i) for i in wide for f in (score, grad)]
        vector = [functools.partial(f, i) for f in (shift, expo, finish) for i in each]
        after = [functools.partial(f, i) for i in wide for f in (value, key)]
        after += [functools.partial(query, pair) for pair in range(2)]
        return before, vector, after

    tiles = [tile(i) for i in range(HEADS_STEP // 2)]
    for piece in tiles[0][0]:
        piece()
    for i in range(len(tiles) + 1):
        mxu = list(tiles[i - 1][2]) if i > 0 else []
        mxu += list(tiles[i + 1][0]) if i + 1 < len(tiles) else []
        vec = list(tiles[i][1]) if i < len(tiles) else []
        rate = max(1, len(vec))
        done = 0
        for n, piece in enumerate(vec):
            want = (n + 1) * len(mxu) // rate
            for m in mxu[done:want]:
                m()
            done = want
            piece()
        for m in mxu[done:]:
            m()

    @pl.when(step == pl.num_programs(0) - 1)
    def _():
        for d in range(n_chunk):
            rows = slice(d * tok, (d + 1) * tok)
            dk = dk_even[rows, :DK] + dk_odd[rows, SHIFT:]
            dkv_refs[d][:, :DV] = dv_acc[rows, :].astype(jnp.bfloat16)
            dkv_refs[d][:, DV:] = (dk * score_scale).astype(jnp.bfloat16)


def run_group(group, sink, q, do, bias, chunks, dq_prev):
    n_chunk = len(chunks)
    tok = q.shape[0]
    heads = sink.shape[0] // G
    steps = heads // HEADS_STEP
    keys = n_chunk * tok
    q_cols, do_cols = HEADS_STEP * DK, HEADS_STEP * DV
    whole = lambda shape: pl.BlockSpec(shape, lambda s: (0,) * len(shape))
    at_group = lambda s: (0, group * steps + s)
    has_prev = dq_prev is not None
    in_specs = [
        pl.BlockSpec(memory_space=pltpu.SMEM),
        pl.BlockSpec((tok, q_cols), at_group),
        pl.BlockSpec((tok, do_cols), at_group),
        pl.BlockSpec((None, keys, tok), lambda s: (group, 0, 0)),
    ] + [whole((tok, DV + DK))] * n_chunk
    args = [sink, q, do, bias] + list(chunks)
    aliases = {}
    if has_prev:
        in_specs.append(pl.BlockSpec(memory_space=pl.ANY))
        args.append(dq_prev)
        aliases = {len(args) - 1: 0}
    out = pl.pallas_call(
        functools.partial(group_kernel, n_chunk, group * heads, has_prev),
        grid=(steps,),
        in_specs=in_specs,
        out_specs=[pl.BlockSpec((tok, q_cols), at_group)]
        + [whole((tok, DV + DK))] * n_chunk
        + [whole((1, heads, tok))],
        out_shape=[jax.ShapeDtypeStruct(q.shape, jnp.bfloat16)]
        + [jax.ShapeDtypeStruct((tok, DV + DK), jnp.bfloat16)] * n_chunk
        + [jax.ShapeDtypeStruct((1, heads, tok), jnp.float32)],
        scratch_shapes=[
            pltpu.VMEM((keys, WIDE), jnp.bfloat16),
            pltpu.VMEM((keys, WIDE), jnp.bfloat16),
            pltpu.VMEM((keys, DV), jnp.bfloat16),
            pltpu.VMEM((keys, WIDE), jnp.float32),
            pltpu.VMEM((keys, WIDE), jnp.float32),
            pltpu.VMEM((keys, DV), jnp.float32),
        ],
        input_output_aliases=aliases,
        cost_estimate=pl.CostEstimate(
            flops=2 * keys * tok * heads * (3 * DK + 2 * DV),
            transcendentals=keys * tok * heads,
            bytes_accessed=tok * heads * (4 * DK + 2 * DV) + keys * tok * 4,
        ),
        compiler_params=pltpu.CompilerParams(vmem_limit_bytes=VMEM_GROUP),
    )(*args)
    return out[0], out[1 : 1 + n_chunk], out[1 + n_chunk]


def make_bias(selection, here, n_ctx, tok):
    blocks, groups, slots = selection.shape
    per = tok // BLK
    dist = jnp.arange(n_ctx, dtype=jnp.int32)
    key_block = (here - dist)[:, None] * per + jnp.arange(per, dtype=jnp.int32)[None, :]
    query_block = here * per + jnp.arange(blocks, dtype=jnp.int32)
    slot_ok = jnp.arange(slots, dtype=jnp.int32)[None, :] < jnp.minimum(slots, query_block + 1)[:, None]
    hit = selection[None, None] == key_block[:, :, None, None, None]
    chosen = jnp.any(hit & slot_ok[None, None, :, None, :], axis=-1)
    chosen = jnp.transpose(chosen, (3, 0, 1, 2))
    chosen = jnp.broadcast_to(
        chosen[:, :, :, None, :, None], (groups, n_ctx, per, BLK, blocks, BLK)
    ).reshape(groups, n_ctx * tok, blocks * BLK)
    key_pos = ((here - dist)[:, None] * tok + jnp.arange(tok, dtype=jnp.int32)[None, :]).reshape(-1)
    query_pos = here * tok + jnp.arange(tok, dtype=jnp.int32)
    causal = key_pos[:, None] <= query_pos[None, :]
    return jnp.where(chosen & causal[None], 0.0, OFF).astype(jnp.float32)


def split_kernel(k_ref, v_ref, *own_refs):
    for g, own in enumerate(own_refs):
        own[:, :DV] = v_ref[:, g * DV : (g + 1) * DV]
        own[:, DV:] = k_ref[:, g * DK : (g + 1) * DK]


def split_groups(k, v):
    tok = k.shape[0]
    return pl.pallas_call(
        split_kernel,
        out_shape=[jax.ShapeDtypeStruct((tok, DV + DK), k.dtype)] * G,
        compiler_params=pltpu.CompilerParams(vmem_limit_bytes=VMEM_SMALL),
        name="split_groups",
    )(k, v)


def join_kernel(n_chunk, *refs):
    parts, (k_ref, v_ref) = refs[: G * n_chunk], refs[G * n_chunk :]
    for g in range(G):
        total = parts[g * n_chunk][...].astype(jnp.float32)
        for d in range(1, n_chunk):
            total += parts[g * n_chunk + d][...].astype(jnp.float32)
        total = total.astype(k_ref.dtype)
        v_ref[:, g * DV : (g + 1) * DV] = total[:, :DV]
        k_ref[:, g * DK : (g + 1) * DK] = total[:, DV:]


def join_groups(parts):
    tok = parts[0][0].shape[0]
    return pl.pallas_call(
        functools.partial(join_kernel, len(parts[0])),
        out_shape=[
            jax.ShapeDtypeStruct((tok, G * DK), jnp.bfloat16),
            jax.ShapeDtypeStruct((tok, G * DV), jnp.bfloat16),
        ],
        compiler_params=pltpu.CompilerParams(vmem_limit_bytes=VMEM_SMALL),
        name="join_groups",
    )(*[x for group in parts for x in group])


def sink_sum(x, sizes):
    for axis, size in sizes:
        hop = 1
        while hop < size:
            other = lax.ppermute(x, axis, [(i, i ^ hop) for i in range(size)])
            x = x + other
            hop *= 2
    return x


def local(n_dp, n_ctx, query_states, key_states, value_states, output_grads, selection, sink_logit):
    tok = query_states.shape[1]
    here = lax.axis_index("ctx")
    q, k, v, do = query_states[0], key_states[0], value_states[0], output_grads[0]
    chunks = [[own] for own in split_groups(k, v)]
    for g in range(G):
        for d in range(1, n_ctx):
            chunks[g].append(
                lax.ppermute(chunks[g][0], "ctx", [(i, i + d) for i in range(n_ctx - d)])
            )
    bias = make_bias(selection[0], here, n_ctx, tok)
    dq = None
    parts, sinks = [], []
    for g in range(G):
        dq, made, sink = run_group(g, sink_logit, q, do, bias, chunks[g], dq)
        back = [made[0]]
        for d in range(1, n_ctx):
            back.append(
                lax.ppermute(made[d], "ctx", [(i, i - d) for i in range(d, n_ctx)])
            )
        parts.append(back)
        sinks.append(sink)
    sink = jnp.sum(jnp.concatenate(sinks, axis=1), axis=(0, 2))
    sink = sink_sum(sink, (("dp", n_dp), ("ctx", n_ctx)))
    key_grad, value_grad = join_groups(parts)
    return dq[None], key_grad[None], value_grad[None], sink


def solution(mesh):
    placed = (
        P("dp", "ctx", None),
        P("dp", "ctx", None),
        P("dp", "ctx", None),
        P("dp", "ctx", None),
        P("dp", "ctx", None, None),
        P(),
    )
    n_ctx = mesh.shape["ctx"]
    return jax.shard_map(
        functools.partial(local, mesh.shape["dp"], n_ctx),
        mesh=mesh,
        in_specs=placed,
        out_specs=(P("dp", "ctx", None), P("dp", "ctx", None), P("dp", "ctx", None), P()),
        check_vma=False,
    )
```
